256 devices in a mesh: leaf: 32 (over z, x), gx: 2 (over core), gy: 4 (over y).
Axes of the slice: x: 4, y: 4, z: 8, core: 2. Of those that a mesh axis runs over, the one named last changes fastest.
Arguments:
- leaf_rhs: float32 [32, 2, 4, 48, 16, 128], P('leaf', 'gx', 'gy'), may hold values from -6 to 6
- leaf_inv: float32 [32, 2, 4, 48, 128, 128], P('leaf', 'gx', 'gy'), may hold values from -0.4 to 1.7
- edge_blocks: float32 [32, 2, 4, 48, 2, 128, 128], P('leaf', 'gx', 'gy'), may hold values from -0.09375 to 0.09375
- edge_target: int32 [32, 2, 4, 48, 2], P('leaf', 'gx', 'gy'), may hold values from 0 to 639
- sep_rhs: float32 [32, 2, 4, 4, 16, 128], P('leaf', 'gx', 'gy'), may hold values from -6 to 6
- sep_inv: float32 [32, 2, 4, 4, 128, 128], P('leaf', 'gx', 'gy'), may hold values from -0.4 to 1.7
- sep_up: float32 [32, 2, 4, 4, 128, 128], P('leaf', 'gx', 'gy'), may hold values from -0.4375 to 0.4375
- sep_parent: int32 [32, 2, 4, 4], P('leaf', 'gx', 'gy'), may hold values from 0 to 3
Outputs:
- leaf_solution: float32 [32, 2, 4, 48, 16, 128], P('leaf', 'gx', 'gy')
- sep_solution: float32 [32, 2, 4, 4, 16, 128], P('leaf', 'gx', 'gy')
The draws below stay inside these ranges and needn't reach their ends.
All inputs are finite; a program needn't handle non-finite values.
Results may differ from the reference program's by a relative error of at most 0.0003.
Values sent between devices are 32-bit elements; how exact they have to be, the bound alone decides.
No kernel may reach another device: no remote copies, remote signals or barrier semaphores. Data moves between devices by JAX's collectives and lax.ppermute only.
A program may use at most 64 MiB of HBM per device.

```python
import math
import jax
import jax.numpy as jnp
from jax import lax

W = 128
R = 16
NS = 48
K = 2
SEP = 4
LEVELS = 32
GRID_X = 2
GRID_Y = 4
TARGETS = 640


def inverse_block(key, shape):
    key_diagonal, key_noise = jax.random.split(key)
    block_width = shape[-1]
    identity = jnp.eye(block_width, dtype=jnp.float32)
    diagonal = jax.random.uniform(key_diagonal, shape[:-1], jnp.float32, 0.7, 1.3)
    off_part = 0.5 * jax.random.truncated_normal(key_noise, -4.0, 4.0, shape, jnp.float32) / math.sqrt(block_width)
    return diagonal[..., None] * identity + off_part


def draw_leaf_inv(key, part):
    return inverse_block(jax.random.fold_in(key, 11), (LEVELS, GRID_X, GRID_Y, NS, W, W))


def draw_sep_inv(key, part):
    return inverse_block(jax.random.fold_in(key, 23), (LEVELS, GRID_X, GRID_Y, SEP, W, W))


def plant(drawn, own_key, least, top_value):
    longest = drawn.shape.index(max(drawn.shape))
    spots = []
    for shift in (0, 1):
        where = [jax.random.randint(jax.random.fold_in(own_key, axis), (), 0, length) for axis, length in enumerate(drawn.shape)]
        where[longest] = (where[longest] + shift) % drawn.shape[longest]
        spots.append(tuple(where))
    return drawn.at[spots[0]].set(least).at[spots[1]].set(top_value)


def block_scale(own_key, dims, cuts, least, top_value):
    def one(position, shards_of):
        steps = jax.random.uniform(jax.random.fold_in(jax.random.fold_in(own_key, 6), position), (shards_of,), jnp.float32, least / len(cuts), top_value / len(cuts))
        return jnp.repeat(jnp.exp(steps), dims[position] // shards_of).reshape((-1,) + (1,) * (len(dims) - position - 1))

    factor_of = one(*cuts[0])
    for cut in cuts[1:]:
        factor_of = factor_of * one(*cut)
    return factor_of


def gaussian(key, extent, width, most, pieces=(), kind=jnp.bfloat16):
    level = block_scale(key, extent, pieces, -0.22, 0.18) if pieces else 1.0
    result = jax.random.normal(key, extent, jnp.float32) * width * level
    return jnp.minimum(jnp.maximum(result, -most), most).astype(kind)


def setup_inputs(seed: int = 0) -> dict:
    splits = jax.random.split(jax.random.key(seed), 9)
    leaf_rhs = gaussian(splits[0], (LEVELS, GRID_X, GRID_Y, NS, R, W), 1.0, 6.0, ((0, 32), (1, 2), (2, 4)), jnp.float32)
    leaf_inv = draw_leaf_inv(jax.random.fold_in(splits[8], 71), 0)
    edge_blocks = gaussian(splits[2], (LEVELS, GRID_X, GRID_Y, NS, K, W, W), (32 * W) ** -0.5, 0.09375, ((0, 32), (1, 2), (2, 4)), jnp.float32)
    edge_target = plant(jax.random.randint(splits[3], (LEVELS, GRID_X, GRID_Y, NS, K), 0, TARGETS), jax.random.fold_in(splits[3], 1), 0, TARGETS - 1).astype(jnp.int32)
    sep_rhs = gaussian(splits[4], (LEVELS, GRID_X, GRID_Y, SEP, R, W), 1.0, 6.0, ((0, 32), (1, 2), (2, 4)), jnp.float32)
    sep_inv = draw_sep_inv(jax.random.fold_in(splits[8], 71), 0)
    sep_up = gaussian(splits[6], (LEVELS, GRID_X, GRID_Y, SEP, W, W), (25 * W // 16) ** -0.5, 0.4375, ((0, 32), (1, 2), (2, 4)), jnp.float32)
    sep_parent = plant(jax.random.randint(splits[7], (LEVELS, GRID_X, GRID_Y, SEP), 0, SEP), jax.random.fold_in(splits[7], 1), 0, SEP - 1).astype(jnp.int32)
    return {"leaf_rhs": leaf_rhs, "leaf_inv": leaf_inv, "edge_blocks": edge_blocks, "edge_target": edge_target, "sep_rhs": sep_rhs, "sep_inv": sep_inv, "sep_up": sep_up, "sep_parent": sep_parent}


HIGHEST = lax.Precision.HIGHEST


def shift_grid(field, step_x, step_y):
    widths = ((1, 1), (1, 1)) + ((0, 0),) * (field.ndim - 2)
    padded = jnp.pad(field, widths)
    return padded[1 + step_x:1 + step_x + GRID_X, 1 + step_y:1 + step_y + GRID_Y]


def reference(leaf_rhs, leaf_inv, edge_blocks, edge_target, sep_rhs, sep_inv, sep_up, sep_parent):
    leaf_mid = jnp.einsum('lxysrw,lxysvw->lxysrv', leaf_rhs, leaf_inv, precision=HIGHEST)
    products = jnp.einsum('lxysrw,lxyskvw->lxyskrv', leaf_mid, edge_blocks, precision=HIGHEST)
    chosen = (edge_target[..., None] == jnp.arange(TARGETS, dtype=jnp.int32)).astype(jnp.float32)
    outgoing = jnp.einsum('lxyskt,lxyskrv->xytrv', chosen, products, precision=HIGHEST)
    outgoing = outgoing.reshape(GRID_X, GRID_Y, 5, LEVELS, SEP, R, W)
    arriving = outgoing[:, :, 0] + shift_grid(outgoing[:, :, 2], -1, 0) + shift_grid(outgoing[:, :, 1], 1, 0)
    arriving = arriving + shift_grid(outgoing[:, :, 4], 0, -1) + shift_grid(outgoing[:, :, 3], 0, 1)
    reduced = sep_rhs - arriving.transpose(2, 0, 1, 3, 4, 5)
    parent_pick = (sep_parent[..., None] == jnp.arange(SEP, dtype=jnp.int32)).astype(jnp.float32)
    incoming = jnp.zeros(sep_rhs.shape[1:], jnp.float32)
    sep_mids = []
    for level_index in range(LEVELS):
        partial_mid = jnp.einsum('xysrw,xysvw->xysrv', reduced[level_index] - incoming, sep_inv[level_index], precision=HIGHEST)
        sep_mids.append(partial_mid)
        lifted = jnp.einsum('xycrw,xycvw->xycrv', partial_mid, sep_up[level_index], precision=HIGHEST)
        incoming = jnp.einsum('xycp,xycrv->xyprv', parent_pick[level_index], lifted, precision=HIGHEST)
    from_above = jnp.zeros(sep_rhs.shape[1:], jnp.float32)
    solved = [None] * LEVELS
    for level_index in range(LEVELS - 1, -1, -1):
        parents = jnp.einsum('xycp,xyprw->xycrw', parent_pick[level_index], from_above, precision=HIGHEST)
        pushed = jnp.einsum('xycrv,xycvw->xycrw', parents, sep_up[level_index], precision=HIGHEST)
        current = jnp.einsum('xysrv,xysvw->xysrw', sep_mids[level_index] - pushed, sep_inv[level_index], precision=HIGHEST)
        solved[level_index] = current
        from_above = current
    sep_solution = jnp.stack(solved)
    by_region = sep_solution.transpose(1, 2, 0, 3, 4, 5)
    solved_table = jnp.stack([by_region, shift_grid(by_region, -1, 0), shift_grid(by_region, 1, 0),
                              shift_grid(by_region, 0, -1), shift_grid(by_region, 0, 1)], axis=2)
    solved_table = solved_table.reshape(GRID_X, GRID_Y, TARGETS, R, W)
    reached = jnp.einsum('lxyskt,xytrw->lxyskrw', chosen, solved_table, precision=HIGHEST)
    pulled_back = jnp.einsum('lxyskrv,lxyskvw->lxysrw', reached, edge_blocks, precision=HIGHEST)
    leaf_solution = jnp.einsum('lxysrv,lxysvw->lxysrw', leaf_mid - pulled_back, leaf_inv, precision=HIGHEST)
    return leaf_solution, sep_solution
```

```python
import functools

import jax
import jax.numpy as jnp
from jax import lax
from jax.experimental import pallas as pl
from jax.experimental.pallas import tpu as pltpu
from jax.sharding import PartitionSpec as P

F32 = jnp.float32
BF16 = jnp.bfloat16
W = 128
R = 16
SEP = 4
NX = 4
NZ = 8
STEP = 4
NN = (((1,), (0,)), ((), ()))
NT = (((1,), (1,)), ((), ()))
TN = (((0,), (0,)), ((), ()))

X_GROUPS = [[z * NX + x for x in range(NX)] for z in range(NZ)]
Z_GROUPS = [[z * NX + x for z in range(NZ)] for x in range(NX)]


def along_x(value, offset):
    pairs = [(z * NX + x, z * NX + (x + offset) % NX) for z in range(NZ) for x in range(NX)]
    return lax.ppermute(value, "leaf", pairs)


def along_z(value, offset):
    pairs = [(z * NX + x, ((z + offset) % NZ) * NX + x) for z in range(NZ) for x in range(NX)]
    return lax.ppermute(value, "leaf", pairs)


def along_y(value, offset):
    count = lax.axis_size("gy")
    return lax.ppermute(value, "gy", [(i, i + offset) for i in range(count) if 0 <= i + offset < count])


def swap_x(value):
    return lax.ppermute(value, "gx", [(0, 1), (1, 0)])


def parts(value):
    high = value.astype(BF16).astype(F32)
    return high, value - high


def rows_of(value):
    return jnp.concatenate(parts(value), axis=0).astype(BF16)


def cols_of(value):
    return jnp.concatenate(parts(value), axis=1).astype(BF16)


def folded(out, rows):
    out = out[:, :W] + out[:, W:]
    return out[:rows] + out[rows:]


def times(left, dims, right):
    out = lax.dot_general(rows_of(left), right, dims, preferred_element_type=F32)
    return folded(out, left.shape[0])


def leaf_up_kernel(idx_ref, own_ref, rhs_ref, inv_ref, edge_ref, sep_ref, mid_ref, prod_ref, acc_ref):
    step = pl.program_id(0)

    @pl.when(step == 0)
    def _():
        acc_ref[...] = jnp.zeros_like(acc_ref)
        for s in range(SEP):
            acc_ref[own_ref[0] * SEP + s] = -sep_ref[s]

    for s in range(STEP):
        mid = times(rhs_ref[s], NT, rows_of(inv_ref[s]))
        mid_ref[s] = mid
        for j in range(2):
            product = times(mid, NT, rows_of(edge_ref[s, j]))
            prod_ref[2 * s + j] = product
            at = idx_ref[(step * STEP + s) * 2 + j]
            acc_ref[at] += product


def leaf_up(idx, own, rhs, inv, edges, sep_rhs):
    count = rhs.shape[0]
    spec = pltpu.PrefetchScalarGridSpec(
        num_scalar_prefetch=2,
        grid=(count // STEP,),
        in_specs=[
            pl.BlockSpec((STEP, R, W), lambda i, *_: (i, 0, 0)),
            pl.BlockSpec((STEP, W, W), lambda i, *_: (i, 0, 0)),
            pl.BlockSpec((STEP, 2, W, W), lambda i, *_: (i, 0, 0, 0)),
            pl.BlockSpec((SEP, R, W), lambda i, *_: (0, 0, 0)),
        ],
        out_specs=[
            pl.BlockSpec((STEP, R, W), lambda i, *_: (i, 0, 0)),
            pl.BlockSpec((2 * STEP, R, W), lambda i, *_: (i, 0, 0)),
            pl.BlockSpec((NX * NZ * SEP + 1, R, W), lambda i, *_: (0, 0, 0)),
        ],
    )
    return pl.pallas_call(
        leaf_up_kernel,
        grid_spec=spec,
        out_shape=[
            jax.ShapeDtypeStruct((count, R, W), F32),
            jax.ShapeDtypeStruct((2 * count, R, W), F32),
            jax.ShapeDtypeStruct((NX * NZ * SEP + 1, R, W), F32),
        ],
        cost_estimate=pl.CostEstimate(flops=10**9, bytes_accessed=12 * 10**6, transcendentals=0),
        name="leaf_up",
    )(idx, own, rhs, inv, edges, sep_rhs)


def collect_kernel(idx_ref, acc_ref, a_ref, b_ref, c_ref, out_ref, sums):
    sums[...] = acc_ref[...]
    count = a_ref.shape[0]

    def add(i, carry):
        for m in range(4):
            n = i * 4 + m
            sums[idx_ref[n]] += a_ref[n]
            sums[idx_ref[count + n]] += b_ref[n]
            sums[idx_ref[2 * count + n]] += c_ref[n]
        return carry

    lax.fori_loop(0, count // 4, add, 0)

    def place(z, carry):
        for k in range(NX * SEP):
            tile = sums[z * NX * SEP + k]
            for x in range(NX):
                out_ref[z * NX + x, k] = tile[4 * x : 4 * x + 4]
        return carry

    lax.fori_loop(0, NZ, place, 0)


def vmem():
    return pl.BlockSpec(memory_space=pltpu.VMEM)


def smem():
    return pl.BlockSpec(memory_space=pltpu.SMEM)


def collect(idx, acc, a, b, c):
    return pl.pallas_call(
        collect_kernel,
        in_specs=[smem()] + [vmem()] * 4,
        out_specs=vmem(),
        out_shape=jax.ShapeDtypeStruct((NX * NZ, NX * SEP, R // NX, W), F32),
        scratch_shapes=[pltpu.VMEM(acc.shape, F32)],
        cost_estimate=pl.CostEstimate(flops=10**6, bytes_accessed=5 * 10**6, transcendentals=0),
        name="collect",
    )(idx, acc, a, b, c)


def picked(rows, c, p):
    return rows[c : c + 1, :] == float(p)


def blocks_kernel(me_ref, p0_ref, p1_ref, p2_ref, p3_ref, bt_ref, bn_ref, g_ref, par_ref, comp_ref):
    me = me_ref[0]
    sources = (p0_ref, p1_ref, p2_ref, p3_ref)
    for o in range(NX):
        level = lax.rem(me - o + NX, NX)
        ref = sources[o]
        for c in range(SEP):
            inv = ref[c * W : (c + 1) * W]
            up = ref[(SEP + c) * W : (SEP + c + 1) * W]
            inv_rows = parts(inv)
            inv_cols = jnp.concatenate(inv_rows, axis=1).astype(BF16)
            normal = times(up, NN, inv_cols)
            bn_ref[level * SEP + c] = cols_of(normal)
            flipped = lax.dot_general(inv_cols, rows_of(up), (((0,), (1,)), ((), ())), preferred_element_type=F32)
            bt_ref[level * SEP + c] = cols_of(folded(flipped, W))
            gram = lax.dot_general(inv_cols, inv_cols, TN, preferred_element_type=F32)
            g_ref[level * SEP + c] = cols_of(folded(gram, W))
        par_ref[level] = ref[2 * SEP * W :]

    def joined(c):
        pair = bn_ref[c].astype(F32)
        return pair[:, :W] + pair[:, W:]

    comp = [joined(c) for c in range(SEP)]
    to = par_ref[0]
    for j in range(1, NX):
        mats = [joined(j * SEP + p) for p in range(SEP)]
        own = par_ref[j]
        following = []
        for c in range(SEP):
            mat = mats[SEP - 1]
            row = own[SEP - 1 : SEP]
            for p in range(SEP - 1):
                mat = jnp.where(picked(to, c, p), mats[p], mat)
                row = jnp.where(picked(to, c, p), own[p : p + 1], row)
            comp[c] = times(mat, NN, cols_of(comp[c]))
            following.append(row)
        to = jnp.concatenate(following + [own[SEP:]], axis=0)
    for c in range(SEP):
        comp_ref[c * W : (c + 1) * W] = comp[c]
    comp_ref[SEP * W :] = to


def blocks(me, p0, p1, p2, p3):
    n = NX * SEP
    return pl.pallas_call(
        blocks_kernel,
        in_specs=[smem()] + [vmem()] * 4,
        out_specs=[vmem()] * 5,
        out_shape=[
            jax.ShapeDtypeStruct((n, W, 2 * W), BF16),
            jax.ShapeDtypeStruct((n, W, 2 * W), BF16),
            jax.ShapeDtypeStruct((n, W, 2 * W), BF16),
            jax.ShapeDtypeStruct((NX, 8, W), F32),
            jax.ShapeDtypeStruct((SEP * W + 8, W), F32),
        ],
        cost_estimate=pl.CostEstimate(flops=10**9, bytes_accessed=5 * 10**6, transcendentals=0),
        name="blocks",
    )(me, p0, p1, p2, p3)


def chain_prep_kernel(*refs):
    ins, (ct_ref, cn_ref, par_ref) = refs[: NZ - 1], refs[NZ - 1 :]
    for o in range(1, NZ):
        ref = ins[o - 1]
        for c in range(SEP):
            mat = ref[c * W : (c + 1) * W]
            cn_ref[o * SEP + c] = cols_of(mat)
            ct_ref[o * SEP + c] = cols_of(mat.T)
        par_ref[o] = ref[SEP * W :]


def chain_prep(others):
    n = NZ * SEP
    return pl.pallas_call(
        chain_prep_kernel,
        in_specs=[vmem()] * (NZ - 1),
        out_specs=[vmem()] * 3,
        out_shape=[
            jax.ShapeDtypeStruct((n, W, 2 * W), BF16),
            jax.ShapeDtypeStruct((n, W, 2 * W), BF16),
            jax.ShapeDtypeStruct((NZ, 8, W), F32),
        ],
        cost_estimate=pl.CostEstimate(flops=10**6, bytes_accessed=6 * 10**6, transcendentals=0),
        name="chain_prep",
    )(*others)


def lift(values, mats, base, parents):
    lifted = [times(values[c], NN, mats[base + c]) for c in range(SEP)]
    sums = []
    for p in range(SEP):
        total = jnp.where(picked(parents, 0, p), lifted[0], 0.0)
        for c in range(1, SEP):
            total = total + jnp.where(picked(parents, c, p), lifted[c], 0.0)
        sums.append(total)
    return sums


def lower(values, mats, base, parents):
    out = []
    for c in range(SEP):
        mine = values[SEP - 1]
        for p in range(SEP - 1):
            mine = jnp.where(picked(parents, c, p), values[p], mine)
        out.append(times(mine, NN, mats[base + c]))
    return out


def gather_kernel(got_ref, bt_ref, par_ref, d_ref, a_ref):
    d = got_ref[0]
    for n in range(1, NX * NZ):
        d = d + got_ref[n]
    d_ref[...] = -d
    incoming = [jnp.zeros((R // NX, W), F32)] * SEP
    for j in range(NX):
        values = [d_ref[j * SEP + c] - incoming[c] for c in range(SEP)]
        incoming = lift(values, bt_ref, j * SEP, par_ref[j])
    for c in range(SEP):
        a_ref[c] = incoming[c]


def up_kernel(me_ref, d_ref, all_ref, ct_ref, cpar_ref, bt_ref, bn_ref, g_ref, par_ref, z_ref, e_ref):
    me = me_ref[0]

    def follow(b, incoming):
        o = me - b
        moved = lift(incoming, ct_ref, o * SEP, cpar_ref[o])
        return [all_ref[b, c] + moved[c] for c in range(SEP)]

    incoming = lax.fori_loop(0, me, follow, [jnp.zeros((R // NX, W), F32)] * SEP)
    for j in range(NX):
        values = [d_ref[j * SEP + c] - incoming[c] for c in range(SEP)]
        for c in range(SEP):
            z_ref[j * SEP + c] = times(values[c], NN, g_ref[j * SEP + c])
        if j < NX - 1:
            incoming = lift(values, bt_ref, j * SEP, par_ref[j])
    above = [z_ref[(NX - 1) * SEP + c] for c in range(SEP)]
    for j in range(NX - 2, -1, -1):
        pushed = lower(above, bn_ref, j * SEP, par_ref[j])
        above = [z_ref[j * SEP + c] - pushed[c] for c in range(SEP)]
    for c in range(SEP):
        e_ref[c] = above[c]


def down_kernel(me_ref, z_ref, all_ref, cn_ref, cpar_ref, bn_ref, par_ref, sol_ref):
    me = me_ref[0]

    def follow(i, above):
        b = NZ - 1 - i
        o = me - b + NZ
        moved = lower(above, cn_ref, o * SEP, cpar_ref[o])
        return [all_ref[b, c] + moved[c] for c in range(SEP)]

    above = lax.fori_loop(0, NZ - 1 - me, follow, [jnp.zeros((R // NX, W), F32)] * SEP)
    for j in range(NX - 1, -1, -1):
        pushed = lower(above, bn_ref, j * SEP, par_ref[j])
        above = [z_ref[j * SEP + c] - pushed[c] for c in range(SEP)]
        for c in range(SEP):
            sol_ref[j * SEP + c] = above[c]


def chain_call(kernel, scalars, name, out_shape, *args):
    return pl.pallas_call(
        kernel,
        in_specs=[smem()] * scalars + [vmem()] * (len(args) - scalars),
        out_specs=jax.tree.map(lambda _: vmem(), out_shape),
        out_shape=out_shape,
        cost_estimate=pl.CostEstimate(flops=10**8, bytes_accessed=4 * 10**6, transcendentals=0),
        name=name,
    )(*args)


def leaf_down_kernel(idx_ref, mid_ref, inv_ref, edge_ref, own_ref, xs_ref, ym_ref, yp_ref, out_ref, table):
    step = pl.program_id(0)

    @pl.when(step == 0)
    def _():
        for n, ref in enumerate((own_ref, xs_ref, ym_ref, yp_ref)):

            def place(z, carry):
                for k in range(NX * SEP):
                    tile = jnp.concatenate([ref[z * NX + x, k] for x in range(NX)], axis=0)
                    table[(n * NZ + z) * NX * SEP + k] = tile
                return carry

            lax.fori_loop(0, NZ, place, 0)
        table[4 * NZ * NX * SEP] = jnp.zeros((R, W), F32)

    for s in range(STEP):
        at = (step * STEP + s) * 2
        pulled = times(table[idx_ref[at]], NN, cols_of(edge_ref[s, 0]))
        pulled = pulled + times(table[idx_ref[at + 1]], NN, cols_of(edge_ref[s, 1]))
        out_ref[s] = times(mid_ref[s] - pulled, NN, cols_of(inv_ref[s]))


def leaf_down(idx, mid, inv, edges, own, xs, ym, yp):
    count = mid.shape[0]
    whole = pl.BlockSpec(own.shape, lambda i, *_: (0, 0, 0, 0), pipeline_mode=pl.Buffered(1))
    spec = pltpu.PrefetchScalarGridSpec(
        num_scalar_prefetch=1,
        grid=(count // STEP,),
        in_specs=[
            pl.BlockSpec((STEP, R, W), lambda i, *_: (i, 0, 0)),
            pl.BlockSpec((STEP, W, W), lambda i, *_: (i, 0, 0)),
            pl.BlockSpec((STEP, 2, W, W), lambda i, *_: (i, 0, 0, 0)),
            whole,
            whole,
            whole,
            whole,
        ],
        out_specs=pl.BlockSpec((STEP, R, W), lambda i, *_: (i, 0, 0)),
        scratch_shapes=[pltpu.VMEM((4 * NZ * NX * SEP + 1, R, W), F32)],
    )
    return pl.pallas_call(
        leaf_down_kernel,
        grid_spec=spec,
        out_shape=jax.ShapeDtypeStruct((count, R, W), F32),
        cost_estimate=pl.CostEstimate(flops=10**9, bytes_accessed=14 * 10**6, transcendentals=0),
        name="leaf_down",
    )(idx, mid, inv, edges, own, xs, ym, yp)


def spread(value, groups=None, count=NX * NZ):
    copies = jnp.broadcast_to(value[None], (count,) + value.shape)
    return lax.all_to_all(copies, "leaf", 0, 0, axis_index_groups=groups)


def local(leaf_rhs, leaf_inv, edge_blocks, edge_target, sep_rhs, sep_inv, sep_up, sep_parent):
    rhs_leaf = leaf_rhs[0, 0, 0]
    inv_leaf = leaf_inv[0, 0, 0]
    blocks_leaf = edge_blocks[0, 0, 0]
    codes = edge_target[0, 0, 0].reshape(-1)
    rhs_sep = sep_rhs[0, 0, 0]
    level = lax.axis_index("leaf").astype(jnp.int32)
    my_x = lax.rem(level, NX).reshape(1)
    my_z = lax.div(level, NX).reshape(1)
    gx = lax.axis_index("gx").astype(jnp.int32)
    gy = lax.axis_index("gy").astype(jnp.int32)
    table = NX * NZ * SEP

    parent_rows = jnp.broadcast_to(sep_parent[0, 0, 0].astype(F32)[:, None], (SEP, W))
    pack = jnp.concatenate(
        [sep_inv[0, 0, 0].reshape(SEP * W, W), sep_up[0, 0, 0].reshape(SEP * W, W), parent_rows, jnp.zeros((8 - SEP, W), F32)],
        axis=0,
    )
    line = [along_x(pack, o) for o in range(1, NX)]
    codes_x = swap_x(codes)
    codes_below = along_y(codes, 1)
    codes_above = along_y(codes, -1)

    def wanted(these, direction):
        return jnp.where(these // table == direction, these % table, table)

    mid, products, acc = leaf_up(wanted(codes, 0), level.reshape(1), rhs_leaf, inv_leaf, blocks_leaf, rhs_sep)
    from_below = along_y(products, 1)
    from_above = along_y(products, -1)
    from_x = swap_x(products)

    bt, bn, gram, par, comp = blocks(my_x, pack, *line)
    others = [along_z(comp, o) for o in range(1, NZ)]
    ct, cn, cpar = chain_prep(others)

    idx = jnp.concatenate([wanted(codes_x, 1 + gx), wanted(codes_below, 4), wanted(codes_above, 3)])
    sums = collect(idx, acc, from_x, from_below, from_above)
    got = lax.all_to_all(sums, "leaf", 0, 0)

    piece = jax.ShapeDtypeStruct((NX * SEP, R // NX, W), F32)
    edge = jax.ShapeDtypeStruct((SEP, R // NX, W), F32)
    d, a = chain_call(gather_kernel, 0, "block_sum", (piece, edge), got, bt, par)
    a_all = spread(a, Z_GROUPS, NZ)
    zs, e = chain_call(up_kernel, 1, "block_up", (piece, edge), my_z, d, a_all, ct, cpar, bt, bn, gram, par)
    e_all = spread(e, Z_GROUPS, NZ)
    sol = chain_call(down_kernel, 1, "block_down", piece, my_z, zs, e_all, cn, cpar, bn, par)
    own = spread(sol)

    below = along_y(own, 1)
    above = along_y(own, -1)
    xs = swap_x(own)
    d_code = codes // table
    slot = jnp.where(d_code == 0, 0, jnp.where(d_code == 2 - gx, 1, jnp.where(d_code == 3, 2, 3)))
    outside = ((d_code == 1) & (gx == 0)) | ((d_code == 2) & (gx == lax.axis_size("gx") - 1))
    outside = outside | ((d_code == 3) & (gy == 0)) | ((d_code == 4) & (gy == lax.axis_size("gy") - 1))
    at = jnp.where(outside, 4 * table, slot * table + codes % table)
    leaf_sol = leaf_down(at, mid, inv_leaf, blocks_leaf, own, xs, below, above)
    mine = lax.dynamic_slice(own, (my_z[0] * NX, my_x[0] * SEP, 0, 0), (NX, SEP, R // NX, W))
    sep_sol = mine.transpose(1, 0, 2, 3).reshape(SEP, R, W)
    return (leaf_sol[None, None, None], sep_sol[None, None, None])


def solution(mesh):
    in_specs = (
        P("leaf", "gx", "gy", None, None, None),
        P("leaf", "gx", "gy", None, None, None),
        P("leaf", "gx", "gy", None, None, None, None),
        P("leaf", "gx", "gy", None, None),
        P("leaf", "gx", "gy", None, None, None),
        P("leaf", "gx", "gy", None, None, None),
        P("leaf", "gx", "gy", None, None, None),
        P("leaf", "gx", "gy", None),
    )
    out_specs = (P("leaf", "gx", "gy", None, None, None), P("leaf", "gx", "gy", None, None, None))
    return jax.shard_map(local, mesh=mesh, in_specs=in_specs, out_specs=out_specs, check_vma=False)
```

```python
import jax
import jax.numpy as jnp
from jax import lax
from jax.experimental import pallas as pl
from jax.experimental.pallas import tpu as pltpu
from jax.sharding import PartitionSpec as P


F32 = jnp.float32
BF16 = jnp.bfloat16
W = 128
R = 16
SEP = 4
NX = 4
NZ = 8
FRONT = NZ // 2
TABLE = NX * NZ * SEP
STEP = 8
NN = (((1,), (0,)), ((), ()))
NT = (((1,), (1,)), ((), ()))
TN = (((0,), (0,)), ((), ()))

Z_GROUPS = [[z * NX + x for z in range(NZ)] for x in range(NX)]


def along_x(value, offset):
    pairs = [(z * NX + x, z * NX + (x + offset) % NX) for z in range(NZ) for x in range(NX)]
    return lax.ppermute(value, "leaf", pairs)


def along_y(value, offset):
    count = lax.axis_size("gy")
    return lax.ppermute(value, "gy", [(i, i + offset) for i in range(count) if 0 <= i + offset < count])


def swap_x(value):
    return lax.ppermute(value, "gx", [(0, 1), (1, 0)])


def parts(value):
    high = value.astype(BF16).astype(F32)
    return high, value - high


def rows_of(value):
    return jnp.concatenate(parts(value), axis=0).astype(BF16)


def cols_of(value):
    return jnp.concatenate(parts(value), axis=1).astype(BF16)


def folded(out, rows):
    out = out[:, :W] + out[:, W:]
    return out[:rows] + out[rows:]


def times(left, dims, right):
    out = lax.dot_general(rows_of(left), right, dims, preferred_element_type=F32)
    return folded(out, left.shape[0])


def leaf_up_kernel(idx_ref, own_ref, rhs_ref, inv_ref, edge_ref, sep_ref, mid_ref, prod_ref, acc_ref):
    step = pl.program_id(0)

    @pl.when(step == 0)
    def _():
        acc_ref[...] = jnp.zeros_like(acc_ref)
        for s in range(SEP):
            acc_ref[own_ref[0] * SEP + s] = -sep_ref[s]

    for s in range(STEP):
        mid = times(rhs_ref[s], NT, rows_of(inv_ref[s]))
        mid_ref[s] = mid
        for j in range(2):
            product = times(mid, NT, rows_of(edge_ref[s, j]))
            prod_ref[2 * s + j] = product
            at = idx_ref[(step * STEP + s) * 2 + j]
            acc_ref[at] += product


def leaf_up(idx, own, rhs, inv, edges, sep_rhs):
    count = rhs.shape[0]
    spec = pltpu.PrefetchScalarGridSpec(
        num_scalar_prefetch=2,
        grid=(count // STEP,),
        in_specs=[
            pl.BlockSpec((STEP, R, W), lambda i, *_: (i, 0, 0)),
            pl.BlockSpec((STEP, W, W), lambda i, *_: (i, 0, 0)),
            pl.BlockSpec((STEP, 2, W, W), lambda i, *_: (i, 0, 0, 0)),
            pl.BlockSpec((SEP, R, W), lambda i, *_: (0, 0, 0)),
        ],
        out_specs=[
            pl.BlockSpec((STEP, R, W), lambda i, *_: (i, 0, 0)),
            pl.BlockSpec((2 * STEP, R, W), lambda i, *_: (i, 0, 0)),
            pl.BlockSpec((NX * NZ * SEP + 1, R, W), lambda i, *_: (0, 0, 0)),
        ],
    )
    return pl.pallas_call(
        leaf_up_kernel,
        grid_spec=spec,
        out_shape=[
            jax.ShapeDtypeStruct((count, R, W), F32),
            jax.ShapeDtypeStruct((2 * count, R, W), F32),
            jax.ShapeDtypeStruct((NX * NZ * SEP + 1, R, W), F32),
        ],
        cost_estimate=pl.CostEstimate(flops=10**9, bytes_accessed=12 * 10**6, transcendentals=0),
        name="leaf_up",
    )(idx, own, rhs, inv, edges, sep_rhs)


def add_list(idx_ref, first, sums, list_ref):
    def add(i, carry):
        for m in range(8):
            n = i * 8 + m
            sums[idx_ref[first + n]] += list_ref[n]
        return carry

    lax.fori_loop(0, list_ref.shape[0] // 8, add, 0)


def collect_x_kernel(idx_ref, acc_ref, a_ref, sums_ref):
    sums_ref[...] = acc_ref[...]
    add_list(idx_ref, 0, sums_ref, a_ref)


def collect_kernel(idx_ref, acc_ref, b_ref, c_ref, out_ref, sums):
    sums[...] = acc_ref[...]
    add_list(idx_ref, 0, sums, b_ref)
    add_list(idx_ref, b_ref.shape[0], sums, c_ref)

    def place(z, carry):
        for k in range(NX * SEP):
            tile = sums[z * NX * SEP + k]
            for x in range(NX):
                out_ref[z * NX + x, k] = tile[4 * x : 4 * x + 4]
        return carry

    lax.fori_loop(0, NZ, place, 0)


def vmem():
    return pl.BlockSpec(memory_space=pltpu.VMEM)


def smem():
    return pl.BlockSpec(memory_space=pltpu.SMEM)


def collect_x(idx, acc, a):
    return pl.pallas_call(
        collect_x_kernel,
        in_specs=[smem(), vmem(), vmem()],
        out_specs=vmem(),
        out_shape=jax.ShapeDtypeStruct(acc.shape, F32),
        cost_estimate=pl.CostEstimate(flops=10**6, bytes_accessed=3 * 10**6, transcendentals=0),
        name="collect_x",
    )(idx, acc, a)


def collect(idx, acc, b, c):
    return pl.pallas_call(
        collect_kernel,
        in_specs=[smem()] + [vmem()] * 3,
        out_specs=vmem(),
        out_shape=jax.ShapeDtypeStruct((NX * NZ, NX * SEP, R // NX, W), F32),
        scratch_shapes=[pltpu.VMEM(acc.shape, F32)],
        cost_estimate=pl.CostEstimate(flops=10**6, bytes_accessed=5 * 10**6, transcendentals=0),
        name="collect",
    )(idx, acc, b, c)


def picked(rows, c, p):
    return rows[c : c + 1, :] == float(p)


def pack_kernel(inv_ref, up_ref, parent_ref, out_ref, gram_ref):
    for c in range(SEP):
        inv_cols = cols_of(inv_ref[c])
        out_ref[c * W : (c + 1) * W] = times(up_ref[c], NN, inv_cols)
        gram = lax.dot_general(inv_cols, inv_cols, TN, preferred_element_type=F32)
        gram_ref[c * W : (c + 1) * W] = folded(gram, W)
    rows = lax.broadcasted_iota(jnp.int32, (8, W), 0)
    parents = jnp.zeros((8, W), F32)
    for c in range(SEP):
        parents = jnp.where(rows == c, parent_ref[c].astype(F32), parents)
    out_ref[SEP * W : SEP * W + 8] = parents


def pack_own(inv, up, parent):
    return pl.pallas_call(
        pack_kernel,
        in_specs=[vmem(), vmem(), smem()],
        out_specs=[vmem()] * 2,
        out_shape=[jax.ShapeDtypeStruct((SEP * W + 8, W), F32), jax.ShapeDtypeStruct((SEP * W, W), F32)],
        cost_estimate=pl.CostEstimate(flops=10**8, bytes_accessed=10**6, transcendentals=0),
        name="pack",
    )(inv, up, parent)


def blocks_kernel(me_ref, p0_ref, p1_ref, p2_ref, p3_ref, bt_ref, bn_ref, par_ref, comp_ref, whole):
    me = me_ref[0]
    for o, ref in enumerate((p0_ref, p1_ref, p2_ref, p3_ref)):
        level = lax.rem(me - o + NX, NX)
        for c in range(SEP):
            mat = ref[c * W : (c + 1) * W]
            bn_ref[level * SEP + c] = cols_of(mat)
            bt_ref[level * SEP + c] = cols_of(mat.T)
        par_ref[level] = ref[SEP * W :]

    def joined(c):
        pair = bn_ref[c].astype(F32)
        return pair[:, :W] + pair[:, W:]

    comp = [joined(c) for c in range(SEP)]
    to = par_ref[0]
    for j in range(1, NX):
        mats = [joined(j * SEP + p) for p in range(SEP)]
        own = par_ref[j]
        following = []
        for c in range(SEP):
            mat = mats[SEP - 1]
            row = own[SEP - 1 : SEP]
            for p in range(SEP - 1):
                mat = jnp.where(picked(to, c, p), mats[p], mat)
                row = jnp.where(picked(to, c, p), own[p : p + 1], row)
            comp[c] = times(mat, NN, cols_of(comp[c]))
            following.append(row)
        to = jnp.concatenate(following + [own[SEP:]], axis=0)
    for c in range(SEP):
        whole[c] = comp[c]
    for n in range(NZ):
        comp_ref[n, :W] = whole[me]
        comp_ref[n, W:] = to


def blocks(me, *line):
    n = NX * SEP
    return pl.pallas_call(
        blocks_kernel,
        in_specs=[smem()] + [vmem()] * len(line),
        out_specs=[vmem()] * 4,
        out_shape=[
            jax.ShapeDtypeStruct((n, W, 2 * W), BF16),
            jax.ShapeDtypeStruct((n, W, 2 * W), BF16),
            jax.ShapeDtypeStruct((NX, 8, W), F32),
            jax.ShapeDtypeStruct((NZ, W + 8, W), F32),
        ],
        scratch_shapes=[pltpu.VMEM((SEP, W, W), F32)],
        cost_estimate=pl.CostEstimate(flops=10**9, bytes_accessed=5 * 10**6, transcendentals=0),
        name="blocks",
    )(me, *line)


def chain_prep_kernel(me_ref, m0_ref, m1_ref, m3_ref, m2a_ref, m2b_ref, *refs):
    grams, (ct_ref, cn_ref, par_ref, g_ref) = refs[:NX], refs[NX:]
    me = me_ref[0]
    for i, sources in enumerate(((m0_ref,), (m1_ref,), (m2a_ref, m2b_ref), (m3_ref,))):
        c = lax.rem(me - i + NX, NX)
        for b in range(NZ):
            ref, at = sources[0], b
            if len(sources) > 1 and at >= FRONT:
                ref, at = sources[1], at - FRONT
            mat = ref[at, :W]
            cn_ref[b * SEP + c] = cols_of(mat)
            ct_ref[b * SEP + c] = cols_of(mat.T)
        for k in range(SEP):
            g_ref[c * SEP + k] = cols_of(grams[i][k * W : (k + 1) * W])
    for b in range(NZ):
        par_ref[b] = m0_ref[b, W:]


def chain_prep(me, *line):
    n = NZ * SEP
    return pl.pallas_call(
        chain_prep_kernel,
        in_specs=[smem()] + [vmem()] * len(line),
        out_specs=[vmem()] * 4,
        out_shape=[
            jax.ShapeDtypeStruct((n, W, 2 * W), BF16),
            jax.ShapeDtypeStruct((n, W, 2 * W), BF16),
            jax.ShapeDtypeStruct((NZ, 8, W), F32),
            jax.ShapeDtypeStruct((NX * SEP, W, 2 * W), BF16),
        ],
        cost_estimate=pl.CostEstimate(flops=10**6, bytes_accessed=6 * 10**6, transcendentals=0),
        name="chain_prep",
    )(me, *line)


def lift(values, mats, base, parents):
    lifted = [times(values[c], NN, mats[base + c]) for c in range(SEP)]
    sums = []
    for p in range(SEP):
        total = jnp.where(picked(parents, 0, p), lifted[0], 0.0)
        for c in range(1, SEP):
            total = total + jnp.where(picked(parents, c, p), lifted[c], 0.0)
        sums.append(total)
    return sums


def lower(values, mats, base, parents):
    out = []
    for c in range(SEP):
        mine = values[SEP - 1]
        for p in range(SEP - 1):
            mine = jnp.where(picked(parents, c, p), values[p], mine)
        out.append(times(mine, NN, mats[base + c]))
    return out


def gather_kernel(got_ref, bt_ref, par_ref, d_ref, a_ref):
    d = got_ref[0]
    for n in range(1, NX * NZ):
        d = d + got_ref[n]
    d_ref[...] = -d
    incoming = [jnp.zeros((R // NX, W), F32)] * SEP
    for j in range(NX):
        values = [d_ref[j * SEP + c] - incoming[c] for c in range(SEP)]
        incoming = lift(values, bt_ref, j * SEP, par_ref[j])
    for c in range(SEP):
        for n in range(NZ):
            a_ref[n, c] = incoming[c]


def up_kernel(me_ref, d_ref, all_ref, ct_ref, cpar_ref, bt_ref, bn_ref, g_ref, par_ref, z_ref, e_ref):
    me = me_ref[0]

    def follow(b, incoming):
        moved = lift(incoming, ct_ref, b * SEP, cpar_ref[b])
        return [all_ref[b, c] + moved[c] for c in range(SEP)]

    incoming = lax.fori_loop(0, me, follow, [jnp.zeros((R // NX, W), F32)] * SEP)
    for j in range(NX):
        values = [d_ref[j * SEP + c] - incoming[c] for c in range(SEP)]
        for c in range(SEP):
            z_ref[j * SEP + c] = times(values[c], NN, g_ref[j * SEP + c])
        if j < NX - 1:
            incoming = lift(values, bt_ref, j * SEP, par_ref[j])
    above = [z_ref[(NX - 1) * SEP + c] for c in range(SEP)]
    for j in range(NX - 2, -1, -1):
        pushed = lower(above, bn_ref, j * SEP, par_ref[j])
        above = [z_ref[j * SEP + c] - pushed[c] for c in range(SEP)]
    for c in range(SEP):
        for n in range(NZ):
            e_ref[n, c] = above[c]


def down_kernel(me_ref, z_ref, all_ref, cn_ref, cpar_ref, bn_ref, par_ref, sol_ref):
    me = me_ref[0]

    def follow(i, above):
        b = NZ - 1 - i
        moved = lower(above, cn_ref, b * SEP, cpar_ref[b])
        return [all_ref[b, c] + moved[c] for c in range(SEP)]

    above = lax.fori_loop(0, NZ - 1 - me, follow, [jnp.zeros((R // NX, W), F32)] * SEP)
    for j in range(NX - 1, -1, -1):
        pushed = lower(above, bn_ref, j * SEP, par_ref[j])
        above = [z_ref[j * SEP + c] - pushed[c] for c in range(SEP)]
        for c in range(SEP):
            for n in range(NX * NZ):
                sol_ref[n, j * SEP + c] = above[c]


def chain_call(kernel, scalars, out_shape, *args):
    return pl.pallas_call(
        kernel,
        in_specs=[smem()] * scalars + [vmem()] * (len(args) - scalars),
        out_specs=jax.tree.map(lambda _: vmem(), out_shape),
        out_shape=out_shape,
        cost_estimate=pl.CostEstimate(flops=10**8, bytes_accessed=4 * 10**6, transcendentals=0),
    )(*args)


def pick_kernel(idx_ref, own_ref, *out_refs):
    count = out_refs[0].shape[0]

    def pick(i, carry):
        for m in range(8):
            n = i * 8 + m
            for k, out_ref in enumerate(out_refs):
                at = idx_ref[k * count + n]
                z, slot = at // (NX * SEP), at % (NX * SEP)
                tile = jnp.concatenate([own_ref[z * NX + x, slot] for x in range(NX)], axis=0)
                out_ref[n] = tile
        return carry

    lax.fori_loop(0, count // 8, pick, 0)


def pick(idx, own, lists):
    count = idx.shape[0] // lists
    return pl.pallas_call(
        pick_kernel,
        in_specs=[smem(), vmem()],
        out_specs=[vmem()] * lists,
        out_shape=[jax.ShapeDtypeStruct((count, R, W), F32)] * lists,
        cost_estimate=pl.CostEstimate(flops=10**6, bytes_accessed=3 * 10**6, transcendentals=0),
        name="pick",
    )(idx, own)


def leaf_down_kernel(slot_ref, mid_ref, inv_ref, edge_ref, *refs):
    lists, out_ref = refs[:-1], refs[-1]
    step = pl.program_id(0)

    def reached(s, j):
        slot = slot_ref[(step * STEP + s) * 2 + j]
        value = jnp.zeros((R, W), F32)
        for n, ref in enumerate(lists):
            value = jnp.where(slot == n, ref[2 * s + j], value)
        return value

    for s in range(STEP):
        pulled = times(reached(s, 0), NN, cols_of(edge_ref[s, 0]))
        pulled = pulled + times(reached(s, 1), NN, cols_of(edge_ref[s, 1]))
        out_ref[s] = times(mid_ref[s] - pulled, NN, cols_of(inv_ref[s]))


def leaf_down(slot, mid, inv, edges, *lists):
    count = mid.shape[0]
    spec = pltpu.PrefetchScalarGridSpec(
        num_scalar_prefetch=1,
        grid=(count // STEP,),
        in_specs=[
            pl.BlockSpec((STEP, R, W), lambda i, *_: (i, 0, 0)),
            pl.BlockSpec((STEP, W, W), lambda i, *_: (i, 0, 0)),
            pl.BlockSpec((STEP, 2, W, W), lambda i, *_: (i, 0, 0, 0)),
        ]
        + [pl.BlockSpec((2 * STEP, R, W), lambda i, *_: (i, 0, 0))] * len(lists),
        out_specs=pl.BlockSpec((STEP, R, W), lambda i, *_: (i, 0, 0)),
    )
    return pl.pallas_call(
        leaf_down_kernel,
        grid_spec=spec,
        out_shape=jax.ShapeDtypeStruct((count, R, W), F32),
        cost_estimate=pl.CostEstimate(flops=10**9, bytes_accessed=14 * 10**6, transcendentals=0),
        name="leaf_down",
    )(slot, mid, inv, edges, *lists)


def exchange(value, groups=None):
    return lax.all_to_all(value, "leaf", 0, 0, axis_index_groups=groups)


def local(leaf_rhs, leaf_inv, edge_blocks, edge_target, sep_rhs, sep_inv, sep_up, sep_parent):
    rhs_leaf = leaf_rhs[0, 0, 0]
    inv_leaf = leaf_inv[0, 0, 0]
    blocks_leaf = edge_blocks[0, 0, 0]
    codes = edge_target[0, 0, 0].reshape(-1)
    rhs_sep = sep_rhs[0, 0, 0]
    level = lax.axis_index("leaf").astype(jnp.int32)
    my_x = lax.rem(level, NX).reshape(1)
    my_z = lax.div(level, NX).reshape(1)
    gx = lax.axis_index("gx").astype(jnp.int32)
    gy = lax.axis_index("gy").astype(jnp.int32)

    own_pack, own_gram = pack_own(sep_inv[0, 0, 0], sep_up[0, 0, 0], sep_parent[0, 0, 0])
    line = [along_x(own_pack, o) for o in range(1, NX)]
    codes_x = swap_x(codes)
    codes_below = along_y(codes, 1)
    codes_above = along_y(codes, -1)

    def wanted(these, direction):
        return jnp.where(these // TABLE == direction, these % TABLE, TABLE)

    mid, products, acc = leaf_up(wanted(codes, 0), level.reshape(1), rhs_leaf, inv_leaf, blocks_leaf, rhs_sep)
    from_below = along_y(products, 1)
    from_above = along_y(products, -1)
    from_x = swap_x(products)

    grams = [own_gram] + [along_x(own_gram, o) for o in range(1, NX)]
    bt, bn, par, comp = blocks(my_x, own_pack, *line)
    columns = exchange(comp, Z_GROUPS)
    before = along_x(columns, 1)
    after = along_x(columns, -1)
    front = along_x(before[:FRONT], 1)
    back = along_x(after[FRONT:], -1)
    ct, cn, cpar, gram = chain_prep(my_x, columns, before, after, front, back, *grams)

    idx_x = wanted(codes_x, 1 + gx)
    idx_y = jnp.concatenate([wanted(codes_below, 4), wanted(codes_above, 3)])
    acc = collect_x(idx_x, acc, from_x)
    sums = collect(idx_y, acc, from_below, from_above)
    got = exchange(sums)

    piece = jax.ShapeDtypeStruct((NX * SEP, R // NX, W), F32)
    copies = jax.ShapeDtypeStruct((NZ, SEP, R // NX, W), F32)
    d, a = chain_call(gather_kernel, 0, (piece, copies), got, bt, par)
    a_all = exchange(a, Z_GROUPS)
    zs, e = chain_call(up_kernel, 1, (piece, copies), my_z, d, a_all, ct, cpar, bt, bn, gram, par)
    e_all = exchange(e, Z_GROUPS)
    sol = jax.ShapeDtypeStruct((NX * NZ, NX * SEP, R // NX, W), F32)
    sol = chain_call(down_kernel, 1, sol, my_z, zs, e_all, cn, cpar, bn, par)
    own = exchange(sol)

    to_below, to_above = pick(jnp.concatenate([idx_y[: codes.size], idx_y[codes.size :]]) % TABLE, own, 2)
    from_above = along_y(to_below, -1)
    from_below = along_y(to_above, 1)
    to_x, mine_list = pick(jnp.concatenate([idx_x, codes]) % TABLE, own, 2)
    from_x = swap_x(to_x)
    d_code = codes // TABLE
    slot = jnp.where(d_code == 0, 0, jnp.where(d_code == 2 - gx, 1, jnp.where(d_code == 3, 2, 3)))
    outside = ((d_code == 1) & (gx == 0)) | ((d_code == 2) & (gx == lax.axis_size("gx") - 1))
    outside = outside | ((d_code == 3) & (gy == 0)) | ((d_code == 4) & (gy == lax.axis_size("gy") - 1))
    slot = jnp.where(outside, 4, slot)
    leaf_sol = leaf_down(slot, mid, inv_leaf, blocks_leaf, mine_list, from_x, from_below, from_above)
    mine = lax.dynamic_slice(own, (my_z[0] * NX, my_x[0] * SEP, 0, 0), (NX, SEP, R // NX, W))
    sep_sol = mine.transpose(1, 0, 2, 3).reshape(SEP, R, W)
    return (leaf_sol[None, None, None], sep_sol[None, None, None])


def solution(mesh):
    in_specs = (
        P("leaf", "gx", "gy", None, None, None),
        P("leaf", "gx", "gy", None, None, None),
        P("leaf", "gx", "gy", None, None, None, None),
        P("leaf", "gx", "gy", None, None),
        P("leaf", "gx", "gy", None, None, None),
        P("leaf", "gx", "gy", None, None, None),
        P("leaf", "gx", "gy", None, None, None),
        P("leaf", "gx", "gy", None),
    )
    out_specs = (P("leaf", "gx", "gy", None, None, None), P("leaf", "gx", "gy", None, None, None))
    return jax.shard_map(local, mesh=mesh, in_specs=in_specs, out_specs=out_specs, check_vma=False)
```

```python
import jax
import jax.numpy as jnp
from jax import lax
from jax.experimental import pallas as pl
from jax.experimental.pallas import tpu as pltpu
from jax.sharding import PartitionSpec as P


F32 = jnp.float32
BF16 = jnp.bfloat16
W = 128
R = 16
SEP = 4
NX = 4
NZ = 8
BEHIND = (1, -1, 3, 4, 2, -3, -2)
FRONT = NZ // 2
TABLE = NX * NZ * SEP
STEP = 12
NN = (((1,), (0,)), ((), ()))
NT = (((1,), (1,)), ((), ()))
TN = (((0,), (0,)), ((), ()))

Z_GROUPS = [[z * NX + x for z in range(NZ)] for x in range(NX)]


def along_x(value, offset):
    pairs = [(z * NX + x, z * NX + (x + offset) % NX) for z in range(NZ) for x in range(NX)]
    return lax.ppermute(value, "leaf", pairs)


def along_z(value, offset):
    pairs = [(z * NX + x, ((z + offset) % NZ) * NX + x) for z in range(NZ) for x in range(NX)]
    return lax.ppermute(value, "leaf", pairs)


def along_y(value, offset):
    count = lax.axis_size("gy")
    return lax.ppermute(value, "gy", [(i, i + offset) for i in range(count) if 0 <= i + offset < count])


def swap_x(value):
    return lax.ppermute(value, "gx", [(0, 1), (1, 0)])


def parts(value):
    high = value.astype(BF16).astype(F32)
    return high, value - high


def halves(value):
    high = value.astype(BF16)
    return high, (value - high.astype(F32)).astype(BF16)


def rows_of(value):
    if value.shape[0] % 16:
        return jnp.concatenate(parts(value), axis=0).astype(BF16)
    return jnp.concatenate(halves(value), axis=0)


def cols_of(value):
    return jnp.concatenate(halves(value), axis=1)


def folded(out, rows):
    out = out[:, :W] + out[:, W:]
    return out[:rows] + out[rows:]


def times(left, dims, right):
    out = lax.dot_general(rows_of(left), right, dims, preferred_element_type=F32)
    return folded(out, left.shape[0])


def leaf_up_kernel(idx_ref, own_ref, rhs_ref, inv_ref, edge_ref, sep_ref, mid_ref, prod_ref, acc_ref):
    step = pl.program_id(0)

    @pl.when(step == 0)
    def _():
        acc_ref[...] = jnp.zeros_like(acc_ref)
        for s in range(SEP):
            acc_ref[own_ref[0] * SEP + s] = -sep_ref[s]

    mids = [times(rhs_ref[s], NT, rows_of(inv_ref[s])) for s in range(STEP)]
    for s in range(STEP):
        mid_ref[s] = mids[s]
    products = [times(mids[s], NT, rows_of(edge_ref[s, j])) for s in range(STEP) for j in range(2)]
    for n in range(2 * STEP):
        prod_ref[n] = products[n]
    for n in range(2 * STEP):
        at = idx_ref[step * STEP * 2 + n]
        acc_ref[at] += products[n]


def leaf_up(idx, own, rhs, inv, edges, sep_rhs):
    count = rhs.shape[0]
    spec = pltpu.PrefetchScalarGridSpec(
        num_scalar_prefetch=2,
        grid=(count // STEP,),
        in_specs=[
            pl.BlockSpec((STEP, R, W), lambda i, *_: (i, 0, 0)),
            pl.BlockSpec((STEP, W, W), lambda i, *_: (i, 0, 0)),
            pl.BlockSpec((STEP, 2, W, W), lambda i, *_: (i, 0, 0, 0)),
            pl.BlockSpec((SEP, R, W), lambda i, *_: (0, 0, 0)),
        ],
        out_specs=[
            pl.BlockSpec((STEP, R, W), lambda i, *_: (i, 0, 0)),
            pl.BlockSpec((2 * STEP, R, W), lambda i, *_: (i, 0, 0)),
            pl.BlockSpec((NX * NZ * SEP + 1, R, W), lambda i, *_: (0, 0, 0)),
        ],
    )
    return pl.pallas_call(
        leaf_up_kernel,
        grid_spec=spec,
        out_shape=[
            jax.ShapeDtypeStruct((count, R, W), F32),
            jax.ShapeDtypeStruct((2 * count + 1, R, W), F32),
            jax.ShapeDtypeStruct((NX * NZ * SEP + 1, R, W), F32),
        ],
        cost_estimate=pl.CostEstimate(flops=10**9, bytes_accessed=12 * 10**6, transcendentals=0),
        name="leaf_up",
    )(idx, own, rhs, inv, edges, sep_rhs)


def add_lists(idx_ref, sums, lists):
    count = idx_ref.shape[0] // len(lists)

    def add(i, carry):
        for m in range(8):
            n = i * 8 + m
            for k, (table, ref) in enumerate(zip(sums, lists)):
                table[idx_ref[k * count + n]] += ref[n]
        return carry

    lax.fori_loop(0, count // 8, add, 0)


def collect_x_kernel(idx_ref, acc_ref, a_ref, sums_ref):
    sums_ref[...] = acc_ref[...]
    add_lists(idx_ref, (sums_ref,), (a_ref,))


def collect_kernel(idx_ref, acc_ref, b_ref, c_ref, out_ref, sums, others):
    sums[...] = acc_ref[...]
    others[...] = jnp.zeros_like(others)
    add_lists(idx_ref, (sums, others), (b_ref, c_ref))

    def place(z, carry):
        for k in range(NX * SEP):
            tile = sums[z * NX * SEP + k] + others[z * NX * SEP + k]
            for x in range(NX):
                out_ref[z * NX + x, k] = tile[4 * x : 4 * x + 4]
        return carry

    lax.fori_loop(0, NZ, place, 0)


def vmem():
    return pl.BlockSpec(memory_space=pltpu.VMEM)


def smem():
    return pl.BlockSpec(memory_space=pltpu.SMEM)


def collect_x(idx, acc, a):
    return pl.pallas_call(
        collect_x_kernel,
        in_specs=[smem(), vmem(), vmem()],
        out_specs=vmem(),
        out_shape=jax.ShapeDtypeStruct(acc.shape, F32),
        cost_estimate=pl.CostEstimate(flops=10**6, bytes_accessed=3 * 10**6, transcendentals=0),
        name="collect_x",
    )(idx, acc, a)


def collect(idx, acc, b, c):
    return pl.pallas_call(
        collect_kernel,
        in_specs=[smem()] + [vmem()] * 3,
        out_specs=vmem(),
        out_shape=jax.ShapeDtypeStruct((NX * NZ, NX * SEP, R // NX, W), F32),
        scratch_shapes=[pltpu.VMEM(acc.shape, F32)] * 2,
        cost_estimate=pl.CostEstimate(flops=10**6, bytes_accessed=5 * 10**6, transcendentals=0),
        name="collect",
    )(idx, acc, b, c)


def picked(rows, c, p):
    return rows[c : c + 1, :] == float(p)


def pack_kernel(inv_ref, up_ref, parent_ref, out_ref, gram_ref):
    for c in range(SEP):
        inv_cols = cols_of(inv_ref[c])
        out_ref[c * W : (c + 1) * W] = times(up_ref[c], NN, inv_cols)
        gram = lax.dot_general(inv_cols, inv_cols, TN, preferred_element_type=F32)
        gram_ref[c * W : (c + 1) * W] = folded(gram, W)
    rows = lax.broadcasted_iota(jnp.int32, (8, W), 0)
    parents = jnp.zeros((8, W), F32)
    for c in range(SEP):
        parents = jnp.where(rows == c, parent_ref[c].astype(F32), parents)
    out_ref[SEP * W : SEP * W + 8] = parents


def pack_own(inv, up, parent):
    return pl.pallas_call(
        pack_kernel,
        in_specs=[vmem(), vmem(), smem()],
        out_specs=[vmem()] * 2,
        out_shape=[jax.ShapeDtypeStruct((SEP * W + 8, W), F32), jax.ShapeDtypeStruct((SEP * W, W), F32)],
        cost_estimate=pl.CostEstimate(flops=10**8, bytes_accessed=10**6, transcendentals=0),
        name="pack",
    )(inv, up, parent)


def blocks_kernel(me_ref, p0_ref, p1_ref, p2_ref, p3_ref, bt_ref, bn_ref, par_ref, comp_ref, whole):
    me = me_ref[0]
    for o, ref in enumerate((p0_ref, p1_ref, p2_ref, p3_ref)):
        level = lax.rem(me - o + NX, NX)
        for c in range(SEP):
            mat = ref[c * W : (c + 1) * W]
            bn_ref[level * SEP + c] = cols_of(mat)
            bt_ref[level * SEP + c] = cols_of(mat.T)
        par_ref[level] = ref[SEP * W :]

    def joined(c):
        pair = bn_ref[c].astype(F32)
        return pair[:, :W] + pair[:, W:]

    comp = [joined(c) for c in range(SEP)]
    to = par_ref[0]
    for j in range(1, NX):
        mats = [joined(j * SEP + p) for p in range(SEP)]
        own = par_ref[j]
        following = []
        for c in range(SEP):
            mat = mats[SEP - 1]
            row = own[SEP - 1 : SEP]
            for p in range(SEP - 1):
                mat = jnp.where(picked(to, c, p), mats[p], mat)
                row = jnp.where(picked(to, c, p), own[p : p + 1], row)
            comp[c] = times(mat, NN, cols_of(comp[c]))
            following.append(row)
        to = jnp.concatenate(following + [own[SEP:]], axis=0)
    for c in range(SEP):
        whole[c] = comp[c]
    comp_ref[:W] = whole[me]
    comp_ref[W:] = to


def blocks(me, *line):
    n = NX * SEP
    return pl.pallas_call(
        blocks_kernel,
        in_specs=[smem()] + [vmem()] * len(line),
        out_specs=[vmem()] * 4,
        out_shape=[
            jax.ShapeDtypeStruct((n, W, 2 * W), BF16),
            jax.ShapeDtypeStruct((n, W, 2 * W), BF16),
            jax.ShapeDtypeStruct((NX, 8, W), F32),
            jax.ShapeDtypeStruct((W + 8, W), F32),
        ],
        scratch_shapes=[pltpu.VMEM((SEP, W, W), F32)],
        cost_estimate=pl.CostEstimate(flops=10**9, bytes_accessed=5 * 10**6, transcendentals=0),
        name="blocks",
    )(me, *line)


def chain_prep_kernel(me_ref, z_ref, m0_ref, m1_ref, m3_ref, m2a_ref, m2b_ref, *refs):
    (g0_ref, g1_ref, g3_ref, g2a_ref, g2b_ref), (ct_ref, cn_ref, par_ref, g_ref) = refs[:5], refs[5:]
    grams = ((g0_ref,), (g1_ref,), (g2a_ref, g2b_ref), (g3_ref,))
    me = me_ref[0]
    for i, sources in enumerate(((m0_ref,), (m1_ref,), (m2a_ref, m2b_ref), (m3_ref,))):
        c = lax.rem(me - i + NX, NX)
        for n, o in enumerate(BEHIND):
            ref, at = sources[0], n
            if len(sources) > 1 and at >= FRONT:
                ref, at = sources[1], at - FRONT
            mat = ref[at * (W + 8) : at * (W + 8) + W]
            b = lax.rem(z_ref[0] - o + NZ, NZ)
            cn_ref[b * SEP + c] = cols_of(mat)
            ct_ref[b * SEP + c] = cols_of(mat.T)
        for k in range(SEP):
            ref, at = grams[i][0], k
            if len(grams[i]) > 1 and at >= SEP // 2:
                ref, at = grams[i][1], at - SEP // 2
            g_ref[c * SEP + k] = cols_of(ref[at * W : (at + 1) * W])
    for n, o in enumerate(BEHIND):
        par_ref[lax.rem(z_ref[0] - o + NZ, NZ)] = m0_ref[n * (W + 8) + W : (n + 1) * (W + 8)]


def chain_prep(me, z, *line):
    n = NZ * SEP
    return pl.pallas_call(
        chain_prep_kernel,
        in_specs=[smem()] * 2 + [vmem()] * len(line),
        out_specs=[vmem()] * 4,
        out_shape=[
            jax.ShapeDtypeStruct((n, W, 2 * W), BF16),
            jax.ShapeDtypeStruct((n, W, 2 * W), BF16),
            jax.ShapeDtypeStruct((NZ, 8, W), F32),
            jax.ShapeDtypeStruct((NX * SEP, W, 2 * W), BF16),
        ],
        cost_estimate=pl.CostEstimate(flops=10**6, bytes_accessed=6 * 10**6, transcendentals=0),
        name="chain_prep",
    )(me, z, *line)


def lift(values, mats, base, parents):
    lifted = [times(values[c], NN, mats[base + c]) for c in range(SEP)]
    sums = []
    for p in range(SEP):
        total = jnp.where(picked(parents, 0, p), lifted[0], 0.0)
        for c in range(1, SEP):
            total = total + jnp.where(picked(parents, c, p), lifted[c], 0.0)
        sums.append(total)
    return sums


def lower(values, mats, base, parents):
    out = []
    for c in range(SEP):
        mine = values[SEP - 1]
        for p in range(SEP - 1):
            mine = jnp.where(picked(parents, c, p), values[p], mine)
        out.append(times(mine, NN, mats[base + c]))
    return out


def gather_kernel(got_ref, bt_ref, par_ref, d_ref, a_ref):
    d = got_ref[0]
    for n in range(1, NX * NZ):
        d = d + got_ref[n]
    d_ref[...] = -d
    incoming = [jnp.zeros((R // NX, W), F32)] * SEP
    for j in range(NX):
        values = [d_ref[j * SEP + c] - incoming[c] for c in range(SEP)]
        incoming = lift(values, bt_ref, j * SEP, par_ref[j])
    for c in range(SEP):
        for n in range(NZ):
            a_ref[n, c] = incoming[c]


def up_kernel(me_ref, d_ref, all_ref, ct_ref, cpar_ref, bt_ref, bn_ref, g_ref, par_ref, z_ref, e_ref):
    me = me_ref[0]

    def follow(b, incoming):
        moved = lift(incoming, ct_ref, b * SEP, cpar_ref[b])
        return [all_ref[b, c] + moved[c] for c in range(SEP)]

    incoming = lax.fori_loop(0, me, follow, [jnp.zeros((R // NX, W), F32)] * SEP)
    for j in range(NX):
        values = [d_ref[j * SEP + c] - incoming[c] for c in range(SEP)]
        for c in range(SEP):
            z_ref[j * SEP + c] = times(values[c], NN, g_ref[j * SEP + c])
        if j < NX - 1:
            incoming = lift(values, bt_ref, j * SEP, par_ref[j])
    above = [z_ref[(NX - 1) * SEP + c] for c in range(SEP)]
    for j in range(NX - 2, -1, -1):
        pushed = lower(above, bn_ref, j * SEP, par_ref[j])
        above = [z_ref[j * SEP + c] - pushed[c] for c in range(SEP)]
    for c in range(SEP):
        for n in range(NZ):
            e_ref[n, c] = above[c]


def down_kernel(me_ref, z_ref, all_ref, cn_ref, cpar_ref, bn_ref, par_ref, sol_ref):
    me = me_ref[0]

    def follow(i, above):
        b = NZ - 1 - i
        moved = lower(above, cn_ref, b * SEP, cpar_ref[b])
        return [all_ref[b, c] + moved[c] for c in range(SEP)]

    above = lax.fori_loop(0, NZ - 1 - me, follow, [jnp.zeros((R // NX, W), F32)] * SEP)
    for j in range(NX - 1, -1, -1):
        pushed = lower(above, bn_ref, j * SEP, par_ref[j])
        above = [z_ref[j * SEP + c] - pushed[c] for c in range(SEP)]
        for c in range(SEP):
            for n in range(NX * NZ):
                sol_ref[n, j * SEP + c] = above[c]


def chain_call(kernel, scalars, out_shape, *args):
    return pl.pallas_call(
        kernel,
        in_specs=[smem()] * scalars + [vmem()] * (len(args) - scalars),
        out_specs=jax.tree.map(lambda _: vmem(), out_shape),
        out_shape=out_shape,
        cost_estimate=pl.CostEstimate(flops=10**8, bytes_accessed=4 * 10**6, transcendentals=0),
    )(*args)


def pick_kernel(idx_ref, own_ref, *out_refs):
    count = out_refs[0].shape[0]

    def pick(i, carry):
        for m in range(8):
            n = i * 8 + m
            for k, out_ref in enumerate(out_refs):
                at = idx_ref[k * count + n]
                z, slot = at // (NX * SEP), at % (NX * SEP)
                tile = jnp.concatenate([own_ref[z * NX + x, slot] for x in range(NX)], axis=0)
                out_ref[n] = tile
        return carry

    lax.fori_loop(0, count // 8, pick, 0)


def pick(idx, own, lists):
    count = idx.shape[0] // lists
    return pl.pallas_call(
        pick_kernel,
        in_specs=[smem(), vmem()],
        out_specs=[vmem()] * lists,
        out_shape=[jax.ShapeDtypeStruct((count, R, W), F32)] * lists,
        cost_estimate=pl.CostEstimate(flops=10**6, bytes_accessed=3 * 10**6, transcendentals=0),
        name="pick",
    )(idx, own)


def leaf_down_kernel(slot_ref, mid_ref, inv_ref, edge_ref, *refs):
    lists, out_ref = refs[:-1], refs[-1]
    step = pl.program_id(0)

    def reached(s, j):
        slot = slot_ref[(step * STEP + s) * 2 + j]
        value = jnp.zeros((R, W), F32)
        for n, ref in enumerate(lists):
            value = jnp.where(slot == n, ref[2 * s + j], value)
        return value

    pulled = [times(reached(s, j), NN, cols_of(edge_ref[s, j])) for s in range(STEP) for j in range(2)]
    rest = [mid_ref[s] - (pulled[2 * s] + pulled[2 * s + 1]) for s in range(STEP)]
    for s in range(STEP):
        out_ref[s] = times(rest[s], NN, cols_of(inv_ref[s]))


def leaf_down(slot, mid, inv, edges, *lists):
    count = mid.shape[0]
    spec = pltpu.PrefetchScalarGridSpec(
        num_scalar_prefetch=1,
        grid=(count // STEP,),
        in_specs=[
            pl.BlockSpec((STEP, R, W), lambda i, *_: (i, 0, 0)),
            pl.BlockSpec((STEP, W, W), lambda i, *_: (i, 0, 0)),
            pl.BlockSpec((STEP, 2, W, W), lambda i, *_: (i, 0, 0, 0)),
        ]
        + [pl.BlockSpec((2 * STEP, R, W), lambda i, *_: (i, 0, 0))] * len(lists),
        out_specs=pl.BlockSpec((STEP, R, W), lambda i, *_: (i, 0, 0)),
    )
    return pl.pallas_call(
        leaf_down_kernel,
        grid_spec=spec,
        out_shape=jax.ShapeDtypeStruct((count, R, W), F32),
        cost_estimate=pl.CostEstimate(flops=10**9, bytes_accessed=14 * 10**6, transcendentals=0),
        name="leaf_down",
    )(slot, mid, inv, edges, *lists)


def exchange(value, groups=None):
    return lax.all_to_all(value, "leaf", 0, 0, axis_index_groups=groups)


def local(leaf_rhs, leaf_inv, edge_blocks, edge_target, sep_rhs, sep_inv, sep_up, sep_parent):
    rhs_leaf = leaf_rhs[0, 0, 0]
    inv_leaf = leaf_inv[0, 0, 0]
    blocks_leaf = edge_blocks[0, 0, 0]
    codes = edge_target[0, 0, 0].reshape(-1)
    rhs_sep = sep_rhs[0, 0, 0]
    level = lax.axis_index("leaf").astype(jnp.int32)
    my_x = lax.rem(level, NX).reshape(1)
    my_z = lax.div(level, NX).reshape(1)
    gx = lax.axis_index("gx").astype(jnp.int32)
    gy = lax.axis_index("gy").astype(jnp.int32)

    own_pack, own_gram = pack_own(sep_inv[0, 0, 0], sep_up[0, 0, 0], sep_parent[0, 0, 0])
    line = [along_x(own_pack, o) for o in range(1, NX)]
    code_block = jnp.broadcast_to(jnp.pad(codes.astype(F32), (0, W - codes.size))[None], (R, W))

    def wanted(these, direction):
        return jnp.where(these // TABLE == direction, these % TABLE, TABLE)

    mid, products, acc = leaf_up(wanted(codes, 0), level.reshape(1), rhs_leaf, inv_leaf, blocks_leaf, rhs_sep)
    products = products.at[codes.size].set(code_block)
    from_below = along_y(products, 1)
    from_above = along_y(products, -1)
    from_x = swap_x(products)

    before = along_x(own_gram, 1)
    after = along_x(own_gram, -1)
    split = SEP // 2 * W
    front = along_x(before[:split], 1)
    back = along_x(after[split:], -1)
    grams = [own_gram, before, after, front, back]
    bt, bn, par, comp = blocks(my_x, own_pack, *line)
    near = [comp, along_z(comp, 1), along_z(comp, -1)]
    far = along_z(jnp.concatenate(near, axis=0), 3)
    columns = near[1:] + [far, along_z(jnp.concatenate(near[:2], axis=0), -3)]
    columns = jnp.concatenate(columns, axis=0)
    before = along_x(columns, 1)
    after = along_x(columns, -1)
    split = FRONT * (W + 8)
    front = along_x(before[:split], 1)
    back = along_x(after[split:], -1)
    ct, cn, cpar, gram = chain_prep(my_x, my_z, columns, before, after, front, back, *grams)


    def codes_of(received):
        return received[codes.size, 0, : codes.size].astype(jnp.int32)

    idx_x = wanted(codes_of(from_x), 1 + gx)
    idx_y = jnp.concatenate([wanted(codes_of(from_below), 4), wanted(codes_of(from_above), 3)])
    acc = collect_x(idx_x, acc, from_x)
    sums = collect(idx_y, acc, from_below, from_above)
    got = exchange(sums)

    piece = jax.ShapeDtypeStruct((NX * SEP, R // NX, W), F32)
    copies = jax.ShapeDtypeStruct((NZ, SEP, R // NX, W), F32)
    d, a = chain_call(gather_kernel, 0, (piece, copies), got, bt, par)
    a_all = exchange(a, Z_GROUPS)
    zs, e = chain_call(up_kernel, 1, (piece, copies), my_z, d, a_all, ct, cpar, bt, bn, gram, par)
    e_all = exchange(e, Z_GROUPS)
    sol = jax.ShapeDtypeStruct((NX * NZ, NX * SEP, R // NX, W), F32)
    sol = chain_call(down_kernel, 1, sol, my_z, zs, e_all, cn, cpar, bn, par)
    own = exchange(sol)

    to_below, to_above = pick(jnp.concatenate([idx_y[: codes.size], idx_y[codes.size :]]) % TABLE, own, 2)
    from_above = along_y(to_below, -1)
    from_below = along_y(to_above, 1)
    to_x, mine_list = pick(jnp.concatenate([idx_x, codes]) % TABLE, own, 2)
    from_x = swap_x(to_x)
    d_code = codes // TABLE
    slot = jnp.where(d_code == 0, 0, jnp.where(d_code == 2 - gx, 1, jnp.where(d_code == 3, 2, 3)))
    outside = ((d_code == 1) & (gx == 0)) | ((d_code == 2) & (gx == lax.axis_size("gx") - 1))
    outside = outside | ((d_code == 3) & (gy == 0)) | ((d_code == 4) & (gy == lax.axis_size("gy") - 1))
    slot = jnp.where(outside, 4, slot)
    leaf_sol = leaf_down(slot, mid, inv_leaf, blocks_leaf, mine_list, from_x, from_below, from_above)
    mine = lax.dynamic_slice(own, (my_z[0] * NX, my_x[0] * SEP, 0, 0), (NX, SEP, R // NX, W))
    sep_sol = mine.transpose(1, 0, 2, 3).reshape(SEP, R, W)
    return (leaf_sol[None, None, None], sep_sol[None, None, None])


def solution(mesh):
    in_specs = (
        P("leaf", "gx", "gy", None, None, None),
        P("leaf", "gx", "gy", None, None, None),
        P("leaf", "gx", "gy", None, None, None, None),
        P("leaf", "gx", "gy", None, None),
        P("leaf", "gx", "gy", None, None, None),
        P("leaf", "gx", "gy", None, None, None),
        P("leaf", "gx", "gy", None, None, None),
        P("leaf", "gx", "gy", None),
    )
    out_specs = (P("leaf", "gx", "gy", None, None, None), P("leaf", "gx", "gy", None, None, None))
    return jax.shard_map(local, mesh=mesh, in_specs=in_specs, out_specs=out_specs, check_vma=False)
```
